32 devices in a mesh: grp: 4 (over z), seq: 8 (over y, x, core).
Axes of the slice: x: 2, y: 2, z: 4, core: 2. Of those that a mesh axis runs over, the one named last changes fastest.
Arguments:
- hidden_in: bfloat16 [24, 4096], P(None, ('grp', 'seq')), may hold values from -6 to 6
- norm_gain: float32 [4096], replicated, may hold values from 0.5 to 1.5
- w_ssm_in: bfloat16 [4096, 8192], P(None, ('grp', 'seq')), may hold values from -0.09375 to 0.09375
- w_ssm_gate: bfloat16 [4096, 8192], P(None, ('grp', 'seq')), may hold values from -0.09375 to 0.09375
- conv_weight: float32 [4, 8192], P(None, ('grp', 'seq')), may hold values from -3 to 3
- conv_bias: float32 [8192], P(('grp', 'seq')), may hold values from -0.5 to 0.5
- conv_state: bfloat16 [24, 3, 8192], P(None, None, ('grp', 'seq')), may hold values from -6 to 6
- w_state_proj: bfloat16 [8192, 288], P(('grp', 'seq')), may hold values from -0.0625 to 0.0625
- w_step: bfloat16 [256, 8192], P(None, ('grp', 'seq')), may hold values from -0.375 to 0.375
- step_bias: float32 [8192], P(('grp', 'seq')), may hold values from -4 to -1
- log_decay: float32 [16, 8192], P(None, ('grp', 'seq')), may hold values from 0 to 2.7
- skip_gain: float32 [8192], P(('grp', 'seq')), may hold values from 0.5 to 1.5
- ssm_state: float32 [24, 16, 8192], P(None, None, ('grp', 'seq')), may hold values from -6 to 6
- w_ssm_out: bfloat16 [8192, 4096], P(('grp', 'seq')), may hold values from -0.125 to 0.125
- w_query: bfloat16 [4096, 2048], P(None, 'grp'), may hold values from -6 to 6
- key_projection: bfloat16 [4096, 1024], P(None, 'grp'), may hold values from -0.09375 to 0.09375
- value_projection: bfloat16 [4096, 1024], P(None, 'grp'), may hold values from -0.09375 to 0.09375
- w_attn_out: bfloat16 [2048, 4096], P('grp', 'seq'), may hold values from -0.125 to 0.125
- w_mlp_gate: bfloat16 [4096, 14336], P(None, ('grp', 'seq')), may hold values from -0.09375 to 0.09375
- w_mlp_up: bfloat16 [4096, 14336], P(None, ('grp', 'seq')), may hold values from -0.09375 to 0.09375
- w_mlp_down: bfloat16 [14336, 4096], P(('grp', 'seq')), may hold values from -0.09375 to 0.09375
- cached_inputs: bfloat16 [24, 512, 4096], P('seq'), may hold values from -6 to 6
- window_lengths: int32 [24], replicated, may hold values from 1 to 512, as said below
Outputs:
- hidden_out: bfloat16 [24, 4096], P(None, ('grp', 'seq'))
- state_out: float32 [24, 16, 8192], P(None, None, ('grp', 'seq'))
The draws below stay inside these ranges and needn't reach their ends.
Inputs may be any that keep to these rules, and one draw needn't show every extreme that they name: `window_lengths`: every sequence has at least one valid cached position, and some sequence fills the whole window of 512.
All inputs are finite; a program needn't handle non-finite values.
Results may differ from the reference program's by a relative error of at most 0.012.
The reference program's roundings to bfloat16 on the way count: a program that leaves them out, or rounds other values in their place, can miss the bound.
Values may be sent and summed in bfloat16 or wider, within the bound.
A program may use at most 128 MiB of HBM per device.

```python
import jax
import jax.numpy as jnp
from jax import lax

MODEL_DIM = 4096
E = 8192
NS = 16
KC = 4
DTR = 256
QUERY_HEADS = 16
KEY_VALUE_HEADS = 8
HEAD_SIZE = 128
FF = 14336
WINDOW_SPAN = 512
BATCH_SEQUENCES = 24


def draw_window_lengths(key, part):
    drawn_lengths = jax.random.randint(jax.random.fold_in(key, 7), (BATCH_SEQUENCES,), 1, WINDOW_SPAN + 1, dtype=jnp.int32)
    chosen = jax.random.randint(jax.random.fold_in(key, 11), (), 0, BATCH_SEQUENCES, dtype=jnp.int32)
    return jnp.where(jnp.arange(BATCH_SEQUENCES, dtype=jnp.int32) == chosen, WINDOW_SPAN, drawn_lengths).astype(jnp.int32)


def draw_w_query(key, part):
    columns = QUERY_HEADS * HEAD_SIZE
    chosen_heads = jax.random.permutation(jax.random.fold_in(key, 3), QUERY_HEADS)
    entries = jax.random.normal(jax.random.fold_in(key, 5), (MODEL_DIM, columns), jnp.float32)
    levels = jnp.array([24.0, 48.0, 96.0], jnp.float32)
    head_scale = jnp.ones((QUERY_HEADS,), jnp.float32).at[chosen_heads[:3]].set(levels)
    column_scale = jnp.repeat(head_scale, HEAD_SIZE)
    scaled = entries * column_scale[None, :] * float(MODEL_DIM) ** (-0.5)
    return jnp.clip(scaled, -6.0, 6.0).astype(jnp.bfloat16)


def spiked(values, key, source, target, blocks, factor):
    def block_of(axis_at):
        return (jnp.arange(values.shape[axis_at]) // (values.shape[axis_at] // blocks)).reshape((-1,) + (1,) * (values.ndim - 1 - axis_at))

    one_side = jax.random.permutation(key, blocks)[block_of(target)]
    far = (block_of(target) + blocks // 2) % blocks
    return jnp.where((block_of(source) == one_side) | (block_of(source) == far), factor * values, values)


def level_of(stream_key, dims, shards, least, high):
    loudness, own = 1.0, jax.random.fold_in(stream_key, 6)
    for dim, shards_of in shards:
        draws = jnp.exp(jax.random.uniform(jax.random.fold_in(own, dim), (shards_of,), jnp.float32, least / len(shards), high / len(shards)))
        loudness = loudness * jnp.repeat(draws, dims[dim] // shards_of).reshape([-1 if axis == dim else 1 for axis in range(len(dims))])
    return loudness


def bell_draw(stream_key, dims, scale, reach, pieces=(), held_as=jnp.bfloat16):
    level = level_of(stream_key, dims, pieces, -0.22, 0.18) if pieces else 1.0
    values = jax.random.normal(stream_key, dims, jnp.float32) * scale * level
    return jnp.minimum(jnp.maximum(values, -reach), reach).astype(held_as)


def noise_with(rng, extent, deviation, limit, shards, heavy, kind=jnp.bfloat16):
    drawn = deviation * jax.random.normal(rng, extent, jnp.float32)
    if shards:
        drawn = drawn * level_of(rng, extent, shards, -0.22, 0.18)
    return jnp.clip(spiked(drawn, jax.random.fold_in(rng, 3), *heavy), -limit, limit).astype(kind)


def setup_inputs(seed: int = 0) -> dict:
    key_list = jax.random.split(jax.random.key(seed), 24)
    return {
        "hidden_in": bell_draw(key_list[0], (BATCH_SEQUENCES, MODEL_DIM), 1.0, 6.0, ((1, 32),)),
        "norm_gain": jnp.clip(1.0 + 0.1 * jax.random.normal(key_list[1], (MODEL_DIM,), jnp.float32), 0.5, 1.5),
        "w_ssm_in": bell_draw(key_list[2], (MODEL_DIM, E), MODEL_DIM ** -0.5, 0.09375, ((1, 32),)),
        "w_ssm_gate": bell_draw(key_list[3], (MODEL_DIM, E), MODEL_DIM ** -0.5, 0.09375, ((1, 32),)),
        "conv_weight": bell_draw(key_list[4], (KC, E), KC ** -0.5, 3.0, ((1, 32),), jnp.float32),
        "conv_bias": jnp.clip(jax.random.uniform(key_list[5], (E,), jnp.float32, -0.5, 0.5) * level_of(key_list[5], (E,), ((0, 32),), -0.4, 0.0), -0.5, 0.5),
        "conv_state": bell_draw(key_list[6], (BATCH_SEQUENCES, KC - 1, E), 1.0, 6.0, ((2, 32),)),
        "w_state_proj": bell_draw(key_list[7], (E, DTR + 2 * NS), E ** -0.5, 0.0625, ((0, 32),)),
        "w_step": bell_draw(key_list[8], (DTR, E), DTR ** -0.5, 0.375, ((1, 32),)),
        "step_bias": jnp.clip(-4.0 + 3.0 * jax.random.uniform(key_list[9], (E,), jnp.float32) ** level_of(key_list[9], (E,), ((0, 32),), -0.2, 0.2), -4.0, -1.0),
        "log_decay": jnp.clip(2.7 * jax.random.uniform(key_list[10], (NS, E), jnp.float32) ** level_of(key_list[10], (NS, E), ((1, 32),), -0.2, 0.2), 0.0, 2.7),
        "skip_gain": jnp.clip(0.5 + 1.0 * jax.random.uniform(key_list[11], (E,), jnp.float32) ** level_of(key_list[11], (E,), ((0, 32),), -0.2, 0.2), 0.5, 1.5),
        "ssm_state": bell_draw(key_list[12], (BATCH_SEQUENCES, NS, E), 1.0, 6.0, ((2, 32),), jnp.float32),
        "w_ssm_out": noise_with(key_list[13], (E, MODEL_DIM), E ** -0.5, 0.125, ((0, 32),), (0, 1, 32, 2.75)),
        "w_query": draw_w_query(jax.random.fold_in(key_list[23], 71), 0),
        "key_projection": bell_draw(key_list[15], (MODEL_DIM, KEY_VALUE_HEADS * HEAD_SIZE), MODEL_DIM ** -0.5, 0.09375, ((1, 4),)),
        "value_projection": bell_draw(key_list[16], (MODEL_DIM, KEY_VALUE_HEADS * HEAD_SIZE), MODEL_DIM ** -0.5, 0.09375, ((1, 4),)),
        "w_attn_out": bell_draw(key_list[17], (QUERY_HEADS * HEAD_SIZE, MODEL_DIM), (QUERY_HEADS * HEAD_SIZE) ** -0.5, 0.125, ((0, 4), (1, 8))),
        "w_mlp_gate": bell_draw(key_list[18], (MODEL_DIM, FF), MODEL_DIM ** -0.5, 0.09375, ((1, 32),)),
        "w_mlp_up": bell_draw(key_list[19], (MODEL_DIM, FF), MODEL_DIM ** -0.5, 0.09375, ((1, 32),)),
        "w_mlp_down": noise_with(key_list[20], (FF, MODEL_DIM), FF ** -0.5, 0.09375, ((0, 32),), (0, 1, 32, 2.75)),
        "cached_inputs": bell_draw(key_list[21], (BATCH_SEQUENCES, WINDOW_SPAN, MODEL_DIM), 1.0, 6.0, ((0, 8),)),
        "window_lengths": draw_window_lengths(jax.random.fold_in(key_list[23], 71), 0),
    }


epsilon = 1e-05
rope_base = 10000.0

def apply_rotary(head_values, positions):
    half_dim = head_values.shape[-1] // 2
    frequency = rope_base ** (-(jnp.arange(half_dim, dtype=jnp.float32) * 2.0) / head_values.shape[-1])
    angles = positions[..., None, None] * frequency
    cosine = jnp.cos(angles)
    sine_part = jnp.sin(angles)
    front_half = head_values[..., :half_dim]
    back_half = head_values[..., half_dim:]
    return jnp.concatenate([front_half * cosine - back_half * sine_part, back_half * cosine + front_half * sine_part], axis=-1)

def reference(hidden_in, norm_gain, w_ssm_in, w_ssm_gate, conv_weight, conv_bias, conv_state, w_state_proj, w_step, step_bias, log_decay, skip_gain, ssm_state, w_ssm_out, w_query, key_projection, value_projection, w_attn_out, w_mlp_gate, w_mlp_up, w_mlp_down, cached_inputs, window_lengths):
    hidden_f = hidden_in.astype(jnp.float32)
    row_scale = lax.rsqrt(lax.optimization_barrier(jnp.mean(hidden_f * hidden_f, axis=1, keepdims=True)) + epsilon)
    normed_input = (hidden_f * row_scale * norm_gain).astype(jnp.bfloat16)
    ssm_input = jnp.dot(normed_input, w_ssm_in, preferred_element_type=jnp.float32).astype(jnp.bfloat16)
    gate_input = jnp.dot(normed_input, w_ssm_gate, preferred_element_type=jnp.float32)
    past_inputs = conv_state.astype(jnp.float32)
    conv_sum = conv_bias + lax.optimization_barrier(jnp.sum(past_inputs * conv_weight[:-1][None], axis=1)) + conv_weight[-1] * lax.optimization_barrier(ssm_input).astype(jnp.float32)
    conv_out = jax.nn.silu(conv_sum)
    low_rank = jnp.dot(conv_out.astype(jnp.bfloat16), w_state_proj, preferred_element_type=jnp.float32)
    step_low = low_rank[:, :DTR].astype(jnp.bfloat16)
    input_map = low_rank[:, DTR:DTR + NS]
    output_map = low_rank[:, DTR + NS:]
    step_size = jax.nn.softplus(jnp.dot(step_low, w_step, preferred_element_type=jnp.float32) + step_bias)
    decay_rate = jnp.exp(log_decay)
    state_out = jnp.exp(-step_size[:, None, :] * decay_rate[None]) * ssm_state + step_size[:, None, :] * input_map[:, :, None] * conv_out[:, None, :]
    ssm_mixed = lax.optimization_barrier(jnp.sum(state_out * output_map[:, :, None], axis=1)) + skip_gain * conv_out
    ssm_gated = (ssm_mixed * jax.nn.silu(gate_input)).astype(jnp.bfloat16)
    ssm_term = jnp.dot(ssm_gated, w_ssm_out, preferred_element_type=jnp.float32)
    gate_act = jnp.dot(normed_input, w_mlp_gate, preferred_element_type=jnp.float32)
    up_act = jnp.dot(normed_input, w_mlp_up, preferred_element_type=jnp.float32)
    mlp_hidden = (jax.nn.silu(gate_act) * up_act).astype(jnp.bfloat16)
    mlp_term = jnp.dot(mlp_hidden, w_mlp_down, preferred_element_type=jnp.float32)
    fresh_position = window_lengths.astype(jnp.float32)
    query = apply_rotary(jnp.dot(normed_input, w_query, preferred_element_type=jnp.float32).reshape(BATCH_SEQUENCES, QUERY_HEADS, HEAD_SIZE), fresh_position).astype(jnp.bfloat16)
    fresh_key = apply_rotary(jnp.dot(normed_input, key_projection, preferred_element_type=jnp.float32).reshape(BATCH_SEQUENCES, KEY_VALUE_HEADS, HEAD_SIZE), fresh_position).astype(jnp.bfloat16)
    fresh_value = jnp.dot(normed_input, value_projection, preferred_element_type=jnp.float32).astype(jnp.bfloat16).reshape(BATCH_SEQUENCES, KEY_VALUE_HEADS, HEAD_SIZE)
    heads_per_group = QUERY_HEADS // KEY_VALUE_HEADS
    attention_scale = HEAD_SIZE ** (-0.5)

    def one_row(row_args):
        window_row_inputs, query_for_row, row_key, row_value, row_length = row_args
        slot_ids = jnp.arange(WINDOW_SPAN, dtype=jnp.int32)
        window_key_rows = jnp.dot(window_row_inputs, key_projection, preferred_element_type=jnp.float32).reshape(WINDOW_SPAN, KEY_VALUE_HEADS, HEAD_SIZE)
        window_key_rows = apply_rotary(window_key_rows, slot_ids.astype(jnp.float32)).astype(jnp.bfloat16)
        window_value_rows = jnp.dot(window_row_inputs, value_projection, preferred_element_type=jnp.float32).astype(jnp.bfloat16).reshape(WINDOW_SPAN, KEY_VALUE_HEADS, HEAD_SIZE)
        grouped_query = query_for_row.astype(jnp.float32).reshape(KEY_VALUE_HEADS, heads_per_group, HEAD_SIZE)
        scores = jnp.einsum('kgd,wkd->kgw', grouped_query, window_key_rows.astype(jnp.float32)) * attention_scale
        fresh_score = jnp.einsum('kgd,kd->kg', grouped_query, row_key.astype(jnp.float32)) * attention_scale
        is_valid = slot_ids < row_length
        scores = jnp.where(is_valid[None, None, :], scores, -1e+30)
        row_max = jnp.maximum(lax.optimization_barrier(jnp.max(scores, axis=-1)), fresh_score)
        weights = jnp.where(is_valid[None, None, :], jnp.exp(scores - row_max[..., None]), 0.0)
        weight_new = jnp.exp(fresh_score - row_max)
        row_total = lax.optimization_barrier(jnp.sum(weights, axis=-1)) + weight_new
        weighted = jnp.einsum('kgw,wkd->kgd', weights, window_value_rows.astype(jnp.float32)) + weight_new[..., None] * row_value.astype(jnp.float32)[:, None, :]
        return (weighted / row_total[..., None]).reshape(QUERY_HEADS * HEAD_SIZE).astype(jnp.bfloat16)
    attended = lax.map(one_row, (cached_inputs, query, fresh_key, fresh_value, window_lengths))
    attn_term = jnp.dot(attended, w_attn_out, preferred_element_type=jnp.float32)
    hidden_out = (hidden_f + (ssm_term + mlp_term + attn_term)).astype(jnp.bfloat16)
    return (hidden_out, state_out)
```

```python
import functools

import jax
import jax.numpy as jnp
from jax import lax
from jax.experimental import pallas as pl
from jax.experimental.pallas import tpu as pltpu
from jax.sharding import PartitionSpec as P

HEAD_SIZE = 128
MESH = pl.DeviceIdType.MESH
VMEM_SPEC = pl.BlockSpec(memory_space=pltpu.VMEM)


epsilon = 1e-05
rope_base = 10000.0


def apply_rotary(head_values, positions):
    half_dim = head_values.shape[-1] // 2
    frequency = rope_base ** (
        -(jnp.arange(half_dim, dtype=jnp.float32) * 2.0) / head_values.shape[-1]
    )
    angles = positions[..., None, None] * frequency
    cosine = jnp.cos(angles)
    sine_part = jnp.sin(angles)
    front_half = head_values[..., :half_dim]
    back_half = head_values[..., half_dim:]
    return jnp.concatenate(
        [front_half * cosine - back_half * sine_part, back_half * cosine + front_half * sine_part],
        axis=-1,
    )


def my_index(seq_size):
    return lax.axis_index("grp") * seq_size + lax.axis_index("seq")


def device_at(index, seq_size):
    return (index // seq_size, index % seq_size)


def meet_all(devices, seq_size):
    me = my_index(seq_size)
    barrier = pltpu.get_barrier_semaphore()

    def greet(k, carry):
        pl.semaphore_signal(
            barrier,
            inc=1,
            device_id=device_at(lax.rem(me + k, devices), seq_size),
            device_id_type=MESH,
        )
        return carry

    lax.fori_loop(1, devices, greet, 0)
    pl.semaphore_wait(barrier, devices - 1)


def each_peer(devices, action):
    def step(k, carry):
        action(k)
        return carry

    lax.fori_loop(1, devices, step, 0)


def norm_gather_kernel(devices, seq_size, x_ref, gain_ref, out_ref, buf, send_sem, recv_sem):
    me = my_index(seq_size)
    width = x_ref.shape[1]
    meet_all(devices, seq_size)

    def copy_for(k):
        return pltpu.make_async_remote_copy(
            src_ref=x_ref,
            dst_ref=buf.at[me],
            send_sem=send_sem.at[k],
            recv_sem=recv_sem.at[k],
            device_id=device_at(lax.rem(me + k, devices), seq_size),
            device_id_type=MESH,
        )

    each_peer(devices, lambda k: copy_for(k).start())
    buf[me] = x_ref[...]
    each_peer(devices, lambda k: copy_for(k).wait())
    total = jnp.zeros(x_ref.shape, jnp.float32)
    for d in range(devices):
        block = buf[d].astype(jnp.float32)
        total = total + block * block
    scale = lax.rsqrt(
        jnp.sum(total, axis=1, keepdims=True) * (1.0 / (devices * width)) + epsilon
    )
    for d in range(devices):
        cols = slice(d * width, (d + 1) * width)
        out_ref[:, cols] = (buf[d].astype(jnp.float32) * scale * gain_ref[:, cols]).astype(
            jnp.bfloat16
        )


def norm_gather(devices, seq_size, hidden_in, norm_gain):
    rows, width = hidden_in.shape
    return pl.pallas_call(
        functools.partial(norm_gather_kernel, devices, seq_size),
        out_shape=jax.ShapeDtypeStruct((rows, devices * width), jnp.bfloat16),
        in_specs=[VMEM_SPEC] * 2,
        out_specs=VMEM_SPEC,
        scratch_shapes=[
            pltpu.VMEM((devices, rows, width), jnp.bfloat16),
            pltpu.SemaphoreType.DMA((devices,)),
            pltpu.SemaphoreType.DMA((devices,)),
        ],
        compiler_params=pltpu.CompilerParams(collective_id=0, has_side_effects=True),
    )(hidden_in, norm_gain.reshape(1, -1))


def sum_gather_kernel(
    devices,
    seq_size,
    part_ref,
    att_ref,
    out_ref,
    att_out_ref,
    split,
    landed,
    reduced,
    full,
    att_buf,
    send_sem,
    recv_sem,
    send_all_sem,
    recv_all_sem,
    att_send_sem,
    att_recv_sem,
):
    me = my_index(seq_size)
    group = lax.axis_index("grp")
    place = lax.axis_index("seq")
    owners, each = split.shape[0], split.shape[1]
    own_rows = att_ref.shape[0]
    for r in range(owners):
        split[r] = part_ref[r * each : (r + 1) * each, :]
    meet_all(devices, seq_size)

    def peer(k):
        return lax.rem(me + k, devices)

    def part_copy(k):
        return pltpu.make_async_remote_copy(
            src_ref=split.at[lax.rem(peer(k), owners)],
            dst_ref=landed.at[me],
            send_sem=send_sem.at[k],
            recv_sem=recv_sem.at[k],
            device_id=device_at(peer(k), seq_size),
            device_id_type=MESH,
        )

    def full_copy(k):
        return pltpu.make_async_remote_copy(
            src_ref=reduced,
            dst_ref=full.at[lax.rem(me, owners)],
            send_sem=send_all_sem.at[k],
            recv_sem=recv_all_sem.at[k],
            device_id=device_at(peer(k), seq_size),
            device_id_type=MESH,
        )

    def att_copy(k):
        return pltpu.make_async_remote_copy(
            src_ref=att_ref,
            dst_ref=att_buf.at[place],
            send_sem=att_send_sem.at[k],
            recv_sem=att_recv_sem.at[k],
            device_id=(group, lax.rem(place + k, seq_size)),
            device_id_type=MESH,
        )

    def start_part(k):
        @pl.when(peer(k) < owners)
        def _():
            part_copy(k).start()

    each_peer(devices, start_part)
    each_peer(seq_size, lambda k: att_copy(k).start())
    att_buf[place] = att_ref[...]

    @pl.when(me < owners)
    def _():
        landed[me] = split[me]
        each_peer(devices, lambda k: part_copy(k).wait_recv())
        total = landed[0]
        for d in range(1, devices):
            total = total + landed[d]
        reduced[...] = total
        full[me] = total
        each_peer(devices, lambda k: full_copy(k).start())

    def end_part(k):
        @pl.when(peer(k) < owners)
        def _():
            part_copy(k).wait_send()

    each_peer(devices, end_part)
    each_peer(seq_size, lambda k: att_copy(k).wait())
    for s in range(seq_size):
        att_out_ref[s * own_rows : (s + 1) * own_rows, :] = att_buf[s]

    def end_full(k):
        @pl.when(lax.rem(me + devices - k, devices) < owners)
        def _():
            full_copy(k).wait_recv()

    each_peer(devices, end_full)

    @pl.when(me < owners)
    def _():
        each_peer(devices, lambda k: full_copy(k).wait_send())

    for r in range(owners):
        out_ref[r * each : (r + 1) * each, :] = full[r]


def sum_gather(devices, seq_size, part, att):
    rows, width = part.shape
    each = -(-rows // devices)
    while rows % each:
        each += 1
    owners = rows // each
    dma = pltpu.SemaphoreType.DMA
    return pl.pallas_call(
        functools.partial(sum_gather_kernel, devices, seq_size),
        out_shape=(
            jax.ShapeDtypeStruct((rows, width), jnp.float32),
            jax.ShapeDtypeStruct((seq_size * att.shape[0], att.shape[1]), jnp.float32),
        ),
        in_specs=[VMEM_SPEC] * 2,
        out_specs=(VMEM_SPEC, VMEM_SPEC),
        scratch_shapes=[
            pltpu.VMEM((owners, each, width), jnp.float32),
            pltpu.VMEM((devices, each, width), jnp.float32),
            pltpu.VMEM((each, width), jnp.float32),
            pltpu.VMEM((owners, each, width), jnp.float32),
            pltpu.VMEM((seq_size,) + att.shape, jnp.float32),
            dma((devices,)),
            dma((devices,)),
            dma((devices,)),
            dma((devices,)),
            dma((seq_size,)),
            dma((seq_size,)),
        ],
        compiler_params=pltpu.CompilerParams(collective_id=1, has_side_effects=True),
    )(part, att)


def scatter_sum_kernel(
    devices, seq_size, term_ref, hidden_ref, out_ref, outgoing, landed, send_sem, recv_sem
):
    me = my_index(seq_size)
    width = hidden_ref.shape[1]
    for d in range(devices):
        outgoing[d] = term_ref[:, d * width : (d + 1) * width].astype(jnp.bfloat16)
    meet_all(devices, seq_size)

    def copy_for(k):
        return pltpu.make_async_remote_copy(
            src_ref=outgoing.at[lax.rem(me + k, devices)],
            dst_ref=landed.at[me],
            send_sem=send_sem.at[k],
            recv_sem=recv_sem.at[k],
            device_id=device_at(lax.rem(me + k, devices), seq_size),
            device_id_type=MESH,
        )

    each_peer(devices, lambda k: copy_for(k).start())
    landed[me] = outgoing[me]
    each_peer(devices, lambda k: copy_for(k).wait())
    total = landed[0].astype(jnp.float32)
    for d in range(1, devices):
        total = total + landed[d].astype(jnp.float32)
    out_ref[...] = (hidden_ref[...].astype(jnp.float32) + total).astype(jnp.bfloat16)


def scatter_sum(devices, seq_size, term, hidden_in):
    rows, width = hidden_in.shape
    return pl.pallas_call(
        functools.partial(scatter_sum_kernel, devices, seq_size),
        out_shape=jax.ShapeDtypeStruct((rows, width), jnp.bfloat16),
        in_specs=[VMEM_SPEC] * 2,
        out_specs=VMEM_SPEC,
        scratch_shapes=[
            pltpu.VMEM((devices, rows, width), jnp.bfloat16),
            pltpu.VMEM((devices, rows, width), jnp.bfloat16),
            pltpu.SemaphoreType.DMA((devices,)),
            pltpu.SemaphoreType.DMA((devices,)),
        ],
        compiler_params=pltpu.CompilerParams(collective_id=2, has_side_effects=True),
    )(term, hidden_in)


def per_device(
    devices,
    seq_size,
    hidden_in,
    norm_gain,
    w_ssm_in,
    w_ssm_gate,
    conv_weight,
    conv_bias,
    conv_state,
    w_state_proj,
    w_step,
    step_bias,
    log_decay,
    skip_gain,
    ssm_state,
    w_ssm_out,
    w_query,
    key_projection,
    value_projection,
    w_attn_out,
    w_mlp_gate,
    w_mlp_up,
    w_mlp_down,
    cached_inputs,
    window_lengths,
):
    batch_rows = hidden_in.shape[0]
    model_width = norm_gain.shape[0]
    normed_input = norm_gather(devices, seq_size, hidden_in, norm_gain)
    ssm_input = jnp.dot(normed_input, w_ssm_in, preferred_element_type=jnp.float32).astype(
        jnp.bfloat16
    )
    gate_input = jnp.dot(normed_input, w_ssm_gate, preferred_element_type=jnp.float32)
    past_inputs = conv_state.astype(jnp.float32)
    conv_sum = (
        conv_bias
        + jnp.sum(past_inputs * conv_weight[:-1][None], axis=1)
        + conv_weight[-1] * lax.optimization_barrier(ssm_input).astype(jnp.float32)
    )
    conv_out = jax.nn.silu(conv_sum)
    rank_size = w_step.shape[0]
    state_size = log_decay.shape[0]
    low_rank_part = jnp.dot(
        conv_out.astype(jnp.bfloat16), w_state_proj, preferred_element_type=jnp.float32
    )
    own_seqs = cached_inputs.shape[0]
    window_size = cached_inputs.shape[1]
    seq_start = lax.axis_index("seq") * own_seqs
    normed_own = lax.dynamic_slice_in_dim(normed_input, seq_start, own_seqs, 0)
    lengths_own = lax.dynamic_slice_in_dim(window_lengths, seq_start, own_seqs, 0)
    heads_here = w_query.shape[1] // HEAD_SIZE
    kv_here = key_projection.shape[1] // HEAD_SIZE
    heads_per_group = heads_here // kv_here
    attention_scale = HEAD_SIZE ** (-0.5)
    fresh_position = lengths_own.astype(jnp.float32)
    query = apply_rotary(
        jnp.dot(normed_own, w_query, preferred_element_type=jnp.float32).reshape(
            own_seqs, heads_here, HEAD_SIZE
        ),
        fresh_position,
    ).astype(jnp.bfloat16)
    fresh_key = apply_rotary(
        jnp.dot(normed_own, key_projection, preferred_element_type=jnp.float32).reshape(
            own_seqs, kv_here, HEAD_SIZE
        ),
        fresh_position,
    ).astype(jnp.bfloat16)
    fresh_value = (
        jnp.dot(normed_own, value_projection, preferred_element_type=jnp.float32)
        .astype(jnp.bfloat16)
        .reshape(own_seqs, kv_here, HEAD_SIZE)
    )
    flat_inputs = cached_inputs.reshape(own_seqs * window_size, model_width)
    slot_ids = jnp.arange(window_size, dtype=jnp.int32)
    positions = jnp.broadcast_to(slot_ids[None, :], (own_seqs, window_size)).astype(jnp.float32)
    window_key_rows = jnp.dot(
        flat_inputs, key_projection, preferred_element_type=jnp.float32
    ).reshape(own_seqs, window_size, kv_here, HEAD_SIZE)
    window_key_rows = apply_rotary(window_key_rows, positions).astype(jnp.bfloat16)
    window_value_rows = (
        jnp.dot(flat_inputs, value_projection, preferred_element_type=jnp.float32)
        .astype(jnp.bfloat16)
        .reshape(own_seqs, window_size, kv_here, HEAD_SIZE)
    )
    grouped_query = query.astype(jnp.float32).reshape(own_seqs, kv_here, heads_per_group, HEAD_SIZE)
    scores = (
        jnp.einsum("bkgd,bpkd->bkgp", grouped_query, window_key_rows.astype(jnp.float32))
        * attention_scale
    )
    fresh_score = (
        jnp.einsum("ynow,ynw->yno", grouped_query, fresh_key.astype(jnp.float32)) * attention_scale
    )
    is_valid = (slot_ids[None, :] < lengths_own[:, None])[:, None, None, :]
    scores = jnp.where(is_valid, scores, -1e30)
    joint_max = jnp.maximum(jnp.max(scores, axis=-1), fresh_score)
    weights = jnp.where(is_valid, jnp.exp(scores - joint_max[..., None]), 0.0)
    weight_new = jnp.exp(fresh_score - joint_max)
    joint_total = jnp.sum(weights, axis=-1) + weight_new
    joint_sum = (
        jnp.einsum("bkgp,bpkd->bkgd", weights, window_value_rows.astype(jnp.float32))
        + weight_new[..., None] * fresh_value.astype(jnp.float32)[:, :, None, :]
    )
    attended_own = (
        (joint_sum / joint_total[..., None])
        .reshape(own_seqs, heads_here * HEAD_SIZE)
        .astype(jnp.bfloat16)
        .astype(jnp.float32)
    )
    low_rank, attended = sum_gather(devices, seq_size, low_rank_part, attended_own)
    step_low = low_rank[:, :rank_size].astype(jnp.bfloat16)
    input_map = low_rank[:, rank_size : rank_size + state_size]
    output_map = low_rank[:, rank_size + state_size :]
    step_size = jax.nn.softplus(
        jnp.dot(step_low, w_step, preferred_element_type=jnp.float32) + step_bias
    )
    decay_rate = jnp.exp(log_decay)
    state_out = (
        jnp.exp(-step_size[:, None, :] * decay_rate[None]) * ssm_state
        + step_size[:, None, :] * input_map[:, :, None] * conv_out[:, None, :]
    )
    ssm_mixed = jnp.sum(state_out * output_map[:, :, None], axis=1) + skip_gain * conv_out
    ssm_gated = (ssm_mixed * jax.nn.silu(gate_input)).astype(jnp.bfloat16)
    ssm_term = jnp.dot(ssm_gated, w_ssm_out, preferred_element_type=jnp.float32)
    gate_act = jnp.dot(normed_input, w_mlp_gate, preferred_element_type=jnp.float32)
    up_act = jnp.dot(normed_input, w_mlp_up, preferred_element_type=jnp.float32)
    mlp_hidden = (jax.nn.silu(gate_act) * up_act).astype(jnp.bfloat16)
    mlp_term = jnp.dot(mlp_hidden, w_mlp_down, preferred_element_type=jnp.float32)
    attn_cols = jnp.dot(attended.astype(jnp.bfloat16), w_attn_out, preferred_element_type=jnp.float32)
    col_start = lax.axis_index("seq") * w_attn_out.shape[1]
    attn_term = lax.dynamic_update_slice(
        jnp.zeros((batch_rows, model_width), jnp.float32), attn_cols, (jnp.int32(0), col_start)
    )
    hidden_out = scatter_sum(devices, seq_size, ssm_term + mlp_term + attn_term, hidden_in)
    return (hidden_out, state_out)


def solution(mesh):
    placed = (
        P(None, ("grp", "seq")),
        P(),
        P(None, ("grp", "seq")),
        P(None, ("grp", "seq")),
        P(None, ("grp", "seq")),
        P(("grp", "seq")),
        P(None, None, ("grp", "seq")),
        P(("grp", "seq"), None),
        P(None, ("grp", "seq")),
        P(("grp", "seq")),
        P(None, ("grp", "seq")),
        P(("grp", "seq")),
        P(None, None, ("grp", "seq")),
        P(("grp", "seq"), None),
        P(None, "grp"),
        P(None, "grp"),
        P(None, "grp"),
        P("grp", "seq"),
        P(None, ("grp", "seq")),
        P(None, ("grp", "seq")),
        P(("grp", "seq"), None),
        P("seq", None, None),
        P(),
    )
    return jax.shard_map(
        functools.partial(per_device, mesh.size, mesh.shape["seq"]),
        mesh=mesh,
        in_specs=placed,
        out_specs=(P(None, ("grp", "seq")), P(None, None, ("grp", "seq"))),
        check_vma=False,
    )
```

```python
import functools

import jax
import jax.numpy as jnp
from jax import lax
from jax.experimental import pallas as pl
from jax.experimental.pallas import tpu as pltpu
from jax.sharding import PartitionSpec as P

HEAD_SIZE = 128
MESH = pl.DeviceIdType.MESH
VMEM_SPEC = pl.BlockSpec(memory_space=pltpu.VMEM)


epsilon = 1e-05
rope_base = 10000.0


def my_index(seq_size):
    return lax.axis_index("grp") * seq_size + lax.axis_index("seq")


def each_peer(groups, seq_size, action):
    group = lax.axis_index("grp")
    place = lax.axis_index("seq")
    group_at = [lax.rem(group + dg, groups) for dg in range(groups)]

    def step(ds, carry):
        there = lax.rem(place + ds, seq_size)
        for dg in range(groups):
            action(dg * seq_size + ds, (group_at[dg], there))
        return carry

    for dg in range(1, groups):
        action(dg * seq_size, (group_at[dg], place))
    lax.fori_loop(1, seq_size, step, 0)


def meet_all(devices, seq_size):
    barrier = pltpu.get_barrier_semaphore()
    each_peer(
        devices // seq_size,
        seq_size,
        lambda k, where: pl.semaphore_signal(
            barrier, inc=1, device_id=where, device_id_type=MESH
        ),
    )
    pl.semaphore_wait(barrier, devices - 1)


def norm_gather_kernel(devices, seq_size, x_ref, gain_ref, out_ref, buf, send_sem, recv_sem):
    me = my_index(seq_size)
    groups = devices // seq_size
    width = x_ref.shape[1]
    meet_all(devices, seq_size)

    def copy_for(k, where):
        return pltpu.make_async_remote_copy(
            src_ref=x_ref,
            dst_ref=buf.at[me],
            send_sem=send_sem.at[k],
            recv_sem=recv_sem.at[k],
            device_id=where,
            device_id_type=MESH,
        )

    each_peer(groups, seq_size, lambda k, where: copy_for(k, where).start())
    buf[me] = x_ref[...]
    each_peer(groups, seq_size, lambda k, where: copy_for(k, where).wait())
    total = jnp.zeros(x_ref.shape, jnp.float32)
    for d in range(devices):
        block = buf[d].astype(jnp.float32)
        total = total + block * block
    scale = lax.rsqrt(
        jnp.sum(total, axis=1, keepdims=True) * (1.0 / (devices * width)) + epsilon
    )
    for d in range(devices):
        cols = slice(d * width, (d + 1) * width)
        out_ref[:, cols] = (buf[d].astype(jnp.float32) * scale * gain_ref[:, cols]).astype(
            jnp.bfloat16
        )


def norm_gather(devices, seq_size, hidden_in, norm_gain):
    rows, width = hidden_in.shape
    return pl.pallas_call(
        functools.partial(norm_gather_kernel, devices, seq_size),
        out_shape=jax.ShapeDtypeStruct((rows, devices * width), jnp.bfloat16),
        in_specs=[VMEM_SPEC] * 2,
        out_specs=VMEM_SPEC,
        scratch_shapes=[
            pltpu.VMEM((devices, rows, width), jnp.bfloat16),
            pltpu.SemaphoreType.DMA((devices,)),
            pltpu.SemaphoreType.DMA((devices,)),
        ],
        compiler_params=pltpu.CompilerParams(
            collective_id=0, has_side_effects=True, vmem_limit_bytes=8 * 1024 * 1024
        ),
        cost_estimate=pl.CostEstimate(
            flops=2_000_000_000, bytes_accessed=30_000_000, transcendentals=0
        ),
    )(hidden_in, norm_gain.reshape(1, -1))


def sum_gather_kernel(
    devices,
    seq_size,
    part_ref,
    att_ref,
    out_ref,
    att_out_ref,
    split,
    landed,
    reduced,
    full,
    att_buf,
    send_sem,
    recv_sem,
    send_all_sem,
    recv_all_sem,
    att_send_sem,
    att_recv_sem,
):
    me = my_index(seq_size)
    groups = devices // seq_size
    group = lax.axis_index("grp")
    place = lax.axis_index("seq")
    owners, each = split.shape[0], split.shape[1]
    own_rows = att_ref.shape[0]
    for r in range(owners):
        split[r] = part_ref[r * each : (r + 1) * each, :]
    meet_all(devices, seq_size)

    def index_of(where):
        return where[0] * seq_size + where[1]

    def part_copy(k, where):
        return pltpu.make_async_remote_copy(
            src_ref=split.at[index_of(where)],
            dst_ref=landed.at[me],
            send_sem=send_sem.at[k],
            recv_sem=recv_sem.at[k],
            device_id=where,
            device_id_type=MESH,
        )

    def land_copy(k, where):
        return pltpu.make_async_remote_copy(
            src_ref=reduced,
            dst_ref=landed.at[me],
            send_sem=send_sem.at[k],
            recv_sem=recv_sem.at[k],
            device_id=where,
            device_id_type=MESH,
        )

    def full_copy(k, where):
        return pltpu.make_async_remote_copy(
            src_ref=reduced,
            dst_ref=full.at[me],
            send_sem=send_all_sem.at[k],
            recv_sem=recv_all_sem.at[k],
            device_id=where,
            device_id_type=MESH,
        )

    def att_copy(k):
        return pltpu.make_async_remote_copy(
            src_ref=att_ref,
            dst_ref=att_buf.at[place],
            send_sem=att_send_sem.at[k],
            recv_sem=att_recv_sem.at[k],
            device_id=(group, lax.rem(place + k, seq_size)),
            device_id_type=MESH,
        )

    def each_place(action):
        def step(k, carry):
            action(k)
            return carry

        lax.fori_loop(1, seq_size, step, 0)

    def start_part(k, where):
        @pl.when(index_of(where) < owners)
        def _():
            part_copy(k, where).start()

    each_peer(groups, seq_size, start_part)
    each_place(lambda k: att_copy(k).start())
    att_buf[place] = att_ref[...]

    @pl.when(me < owners)
    def _():
        landed[me] = split[me]
        each_peer(groups, seq_size, lambda k, where: land_copy(k, where).wait_recv())
        total = landed[0]
        for d in range(1, devices):
            total = total + landed[d]
        reduced[...] = total
        full[me] = total
        each_peer(groups, seq_size, lambda k, where: full_copy(k, where).start())

    def end_part(k, where):
        @pl.when(index_of(where) < owners)
        def _():
            part_copy(k, where).wait_send()

    each_peer(groups, seq_size, end_part)
    each_place(lambda k: att_copy(k).wait())
    for s in range(seq_size):
        att_out_ref[s * own_rows : (s + 1) * own_rows, :] = att_buf[s]

    def end_full(ds, carry):
        there = lax.rem(place + seq_size - ds, seq_size)
        for dg in range(groups):
            source = lax.rem(group + groups - dg, groups) * seq_size + there
            k = dg * seq_size + ds

            @pl.when(jnp.logical_and(source < owners, k > 0))
            def _():
                pltpu.make_async_remote_copy(
                    src_ref=reduced,
                    dst_ref=full.at[source],
                    send_sem=send_all_sem.at[k],
                    recv_sem=recv_all_sem.at[k],
                    device_id=(group, lax.rem(place + 1, seq_size)),
                    device_id_type=MESH,
                ).wait_recv()

        return carry

    lax.fori_loop(0, seq_size, end_full, 0)

    @pl.when(me < owners)
    def _():
        each_peer(groups, seq_size, lambda k, where: full_copy(k, where).wait_send())

    for r in range(owners):
        out_ref[r * each : (r + 1) * each, :] = full[r]


def sum_gather(devices, seq_size, part, att):
    rows, width = part.shape
    each = -(-rows // devices)
    while rows % each:
        each += 1
    owners = rows // each
    dma = pltpu.SemaphoreType.DMA
    return pl.pallas_call(
        functools.partial(sum_gather_kernel, devices, seq_size),
        out_shape=(
            jax.ShapeDtypeStruct((rows, width), jnp.float32),
            jax.ShapeDtypeStruct((seq_size * att.shape[0], att.shape[1]), jnp.float32),
        ),
        in_specs=[VMEM_SPEC] * 2,
        out_specs=(VMEM_SPEC, VMEM_SPEC),
        scratch_shapes=[
            pltpu.VMEM((owners, each, width), jnp.float32),
            pltpu.VMEM((devices, each, width), jnp.float32),
            pltpu.VMEM((each, width), jnp.float32),
            pltpu.VMEM((owners, each, width), jnp.float32),
            pltpu.VMEM((seq_size,) + att.shape, jnp.float32),
            dma((devices,)),
            dma((devices,)),
            dma((devices,)),
            dma((devices,)),
            dma((seq_size,)),
            dma((seq_size,)),
        ],
        compiler_params=pltpu.CompilerParams(
            collective_id=1, has_side_effects=True, vmem_limit_bytes=8 * 1024 * 1024
        ),
        cost_estimate=pl.CostEstimate(
            flops=2_000_000_000, bytes_accessed=30_000_000, transcendentals=0
        ),
    )(part, att)


def scatter_sum_kernel(
    devices, seq_size, term_ref, hidden_ref, out_ref, outgoing, landed, send_sem, recv_sem
):
    me = my_index(seq_size)
    groups = devices // seq_size
    width = hidden_ref.shape[1]
    for d in range(devices):
        outgoing[d] = term_ref[:, d * width : (d + 1) * width].astype(jnp.bfloat16)
    meet_all(devices, seq_size)

    def copy_for(k, where):
        return pltpu.make_async_remote_copy(
            src_ref=outgoing.at[where[0] * seq_size + where[1]],
            dst_ref=landed.at[me],
            send_sem=send_sem.at[k],
            recv_sem=recv_sem.at[k],
            device_id=where,
            device_id_type=MESH,
        )

    each_peer(groups, seq_size, lambda k, where: copy_for(k, where).start())
    landed[me] = outgoing[me]
    each_peer(groups, seq_size, lambda k, where: copy_for(k, where).wait())
    total = landed[0].astype(jnp.float32)
    for d in range(1, devices):
        total = total + landed[d].astype(jnp.float32)
    out_ref[...] = (hidden_ref[...].astype(jnp.float32) + total).astype(jnp.bfloat16)


def scatter_sum(devices, seq_size, term, hidden_in):
    rows, width = hidden_in.shape
    return pl.pallas_call(
        functools.partial(scatter_sum_kernel, devices, seq_size),
        out_shape=jax.ShapeDtypeStruct((rows, width), jnp.bfloat16),
        in_specs=[VMEM_SPEC] * 2,
        out_specs=VMEM_SPEC,
        scratch_shapes=[
            pltpu.VMEM((devices, rows, width), jnp.bfloat16),
            pltpu.VMEM((devices, rows, width), jnp.bfloat16),
            pltpu.SemaphoreType.DMA((devices,)),
            pltpu.SemaphoreType.DMA((devices,)),
        ],
        compiler_params=pltpu.CompilerParams(
            collective_id=2, has_side_effects=True, vmem_limit_bytes=8 * 1024 * 1024
        ),
        cost_estimate=pl.CostEstimate(
            flops=2_000_000_000, bytes_accessed=30_000_000, transcendentals=0
        ),
    )(term, hidden_in)


def window_kernel(
    own,
    kv_here,
    heads_per_group,
    normed_ref,
    cos_ref,
    sin_ref,
    cos_new_ref,
    sin_new_ref,
    bias_ref,
    cached_ref,
    wk_ref,
    wv_ref,
    wq_ref,
    out_ref,
    x_buf,
    wkv,
    wq,
    k_buf,
    v_buf,
    new_rows,
    x_sem,
    w_sem,
):
    tiles, tile = x_buf.shape[0], x_buf.shape[1]
    per_seq = tiles // own
    window = per_seq * tile
    kv_width = kv_here * HEAD_SIZE
    q_width = wq.shape[1]
    copy_k = pltpu.make_async_copy(wk_ref, wkv.at[:, pl.ds(0, kv_width)], w_sem.at[0])
    copy_v = pltpu.make_async_copy(wv_ref, wkv.at[:, pl.ds(kv_width, kv_width)], w_sem.at[1])
    copy_q = pltpu.make_async_copy(wq_ref, wq, w_sem.at[2])
    copy_k.start()
    copy_v.start()
    for t in range(tiles):
        pltpu.make_async_copy(cached_ref.at[t], x_buf.at[t], x_sem.at[t]).start()
    copy_q.start()
    copy_k.wait()
    copy_v.wait()

    def turned(values, cosine, sine):
        return (values * cosine + pltpu.roll(values, HEAD_SIZE // 2, 1) * sine).astype(
            jnp.bfloat16
        )

    def project(t, carry):
        pltpu.make_async_copy(cached_ref.at[t], x_buf.at[t], x_sem.at[t]).wait()
        rows = jnp.dot(x_buf[t], wkv[...], preferred_element_type=jnp.float32)
        slots = pl.ds(pl.multiple_of(lax.rem(t, per_seq) * tile, tile), tile)
        cosine, sine = cos_ref[slots, :], sin_ref[slots, :]
        here = pl.ds(pl.multiple_of(t * tile, tile), tile)
        for h in range(kv_here):
            cols = slice(h * HEAD_SIZE, (h + 1) * HEAD_SIZE)
            k_buf[here, cols] = turned(rows[:, cols], cosine, sine)
        v_buf[here, :] = rows[:, kv_width:].astype(jnp.bfloat16)
        return carry

    lax.fori_loop(0, tiles, project, 0)
    copy_q.wait()
    normed = normed_ref[...]
    new_rows[:, :q_width] = jnp.dot(normed, wq[...], preferred_element_type=jnp.float32)
    new_rows[:, q_width:] = jnp.dot(normed, wkv[...], preferred_element_type=jnp.float32)
    first = lax.axis_index("seq") * own
    scale = HEAD_SIZE ** (-0.5)
    for b in range(own):
        row = new_rows[pl.ds(first + b, 1), :]
        cosine, sine = cos_new_ref[b : b + 1, :], sin_new_ref[b : b + 1, :]
        here = slice(b * window, (b + 1) * window)
        for h in range(kv_here):
            cols = slice(h * HEAD_SIZE, (h + 1) * HEAD_SIZE)
            heads = range(h * heads_per_group, (h + 1) * heads_per_group)
            query = turned(
                jnp.concatenate(
                    [row[:, q * HEAD_SIZE : (q + 1) * HEAD_SIZE] for q in heads], axis=0
                ),
                cosine,
                sine,
            )
            at = q_width + h * HEAD_SIZE
            fresh_key = turned(row[:, at : at + HEAD_SIZE], cosine, sine)
            at += kv_width
            fresh_value = row[:, at : at + HEAD_SIZE].astype(jnp.bfloat16).astype(jnp.float32)
            scores = lax.dot_general(
                query,
                k_buf[here, cols],
                (((1,), (1,)), ((), ())),
                preferred_element_type=jnp.float32,
            )
            scores = scores * scale + bias_ref[b : b + 1, :]
            fresh = (
                jnp.sum(
                    query.astype(jnp.float32) * fresh_key.astype(jnp.float32),
                    axis=1,
                    keepdims=True,
                )
                * scale
            )
            top = jnp.maximum(jnp.max(scores, axis=1, keepdims=True), fresh)
            weights = jnp.exp(scores - top)
            weight_new = jnp.exp(fresh - top)
            total = jnp.sum(weights, axis=1, keepdims=True) + weight_new
            mixed = jnp.dot(
                weights.astype(jnp.bfloat16), v_buf[here, cols], preferred_element_type=jnp.float32
            )
            mixed = (mixed + weight_new * fresh_value) / total
            mixed = mixed.astype(jnp.bfloat16).astype(jnp.float32)
            for i, q in enumerate(heads):
                out_ref[b : b + 1, q * HEAD_SIZE : (q + 1) * HEAD_SIZE] = mixed[i : i + 1, :]


def rotary_tables(positions):
    half_dim = HEAD_SIZE // 2
    frequency = rope_base ** (-(jnp.arange(half_dim, dtype=jnp.float32) * 2.0) / HEAD_SIZE)
    angles = positions[:, None] * frequency
    cosine, sine = jnp.cos(angles), jnp.sin(angles)
    return (
        jnp.concatenate([cosine, cosine], axis=1),
        jnp.concatenate([-sine, sine], axis=1),
    )


def window_attention(normed, cached, wk, wv, wq, lengths):
    own, window, width = cached.shape
    tile = 256 if window % 256 == 0 else window
    tiles = own * window // tile
    kv_width, q_width = wk.shape[1], wq.shape[1]
    slots = jnp.arange(window, dtype=jnp.int32)
    cosine, sine = rotary_tables(slots.astype(jnp.float32))
    cos_new, sin_new = rotary_tables(lengths.astype(jnp.float32))
    bias = jnp.where(slots[None, :] < lengths[:, None], 0.0, -1e30).astype(jnp.float32)
    any_spec = pl.BlockSpec(memory_space=pl.ANY)
    return pl.pallas_call(
        functools.partial(
            window_kernel, own, kv_width // HEAD_SIZE, q_width // kv_width
        ),
        out_shape=jax.ShapeDtypeStruct((own, q_width), jnp.float32),
        in_specs=[VMEM_SPEC] * 6 + [any_spec] * 4,
        out_specs=VMEM_SPEC,
        scratch_shapes=[
            pltpu.VMEM((tiles, tile, width), jnp.bfloat16),
            pltpu.VMEM((width, 2 * kv_width), jnp.bfloat16),
            pltpu.VMEM((width, q_width), jnp.bfloat16),
            pltpu.VMEM((own * window, kv_width), jnp.bfloat16),
            pltpu.VMEM((own * window, kv_width), jnp.bfloat16),
            pltpu.VMEM((normed.shape[0], q_width + 2 * kv_width), jnp.float32),
            pltpu.SemaphoreType.DMA((tiles,)),
            pltpu.SemaphoreType.DMA((3,)),
        ],
        compiler_params=pltpu.CompilerParams(vmem_limit_bytes=48 * 1024 * 1024),
    )(normed, cosine, sine, cos_new, sin_new, bias, cached.reshape(tiles, tile, width), wk, wv, wq)


def per_device(
    devices,
    seq_size,
    hidden_in,
    norm_gain,
    w_ssm_in,
    w_ssm_gate,
    conv_weight,
    conv_bias,
    conv_state,
    w_state_proj,
    w_step,
    step_bias,
    log_decay,
    skip_gain,
    ssm_state,
    w_ssm_out,
    w_query,
    key_projection,
    value_projection,
    w_attn_out,
    w_mlp_gate,
    w_mlp_up,
    w_mlp_down,
    cached_inputs,
    window_lengths,
):
    batch_rows = hidden_in.shape[0]
    model_width = norm_gain.shape[0]
    normed_input = norm_gather(devices, seq_size, hidden_in, norm_gain)
    ssm_input = jnp.dot(normed_input, w_ssm_in, preferred_element_type=jnp.float32).astype(
        jnp.bfloat16
    )
    gate_input = jnp.dot(normed_input, w_ssm_gate, preferred_element_type=jnp.float32)
    past_inputs = conv_state.astype(jnp.float32)
    conv_sum = (
        conv_bias
        + jnp.sum(past_inputs * conv_weight[:-1][None], axis=1)
        + conv_weight[-1] * lax.optimization_barrier(ssm_input).astype(jnp.float32)
    )
    conv_out = jax.nn.silu(conv_sum)
    rank_size = w_step.shape[0]
    state_size = log_decay.shape[0]
    low_rank_part = jnp.dot(
        conv_out.astype(jnp.bfloat16), w_state_proj, preferred_element_type=jnp.float32
    )
    own_seqs = cached_inputs.shape[0]
    seq_start = lax.axis_index("seq") * own_seqs
    lengths_own = lax.dynamic_slice_in_dim(window_lengths, seq_start, own_seqs, 0)
    attended_own = window_attention(
        normed_input, cached_inputs, key_projection, value_projection, w_query, lengths_own
    )
    low_rank, attended = sum_gather(devices, seq_size, low_rank_part, attended_own)
    step_low = low_rank[:, :rank_size].astype(jnp.bfloat16)
    input_map = low_rank[:, rank_size : rank_size + state_size]
    output_map = low_rank[:, rank_size + state_size :]
    step_size = jax.nn.softplus(
        jnp.dot(step_low, w_step, preferred_element_type=jnp.float32) + step_bias
    )
    decay_rate = jnp.exp(log_decay)
    state_out = (
        jnp.exp(-step_size[:, None, :] * decay_rate[None]) * ssm_state
        + step_size[:, None, :] * input_map[:, :, None] * conv_out[:, None, :]
    )
    ssm_mixed = jnp.sum(state_out * output_map[:, :, None], axis=1) + skip_gain * conv_out
    ssm_gated = (ssm_mixed * jax.nn.silu(gate_input)).astype(jnp.bfloat16)
    ssm_term = jnp.dot(ssm_gated, w_ssm_out, preferred_element_type=jnp.float32)
    gate_act = jnp.dot(normed_input, w_mlp_gate, preferred_element_type=jnp.float32)
    up_act = jnp.dot(normed_input, w_mlp_up, preferred_element_type=jnp.float32)
    mlp_hidden = (jax.nn.silu(gate_act) * up_act).astype(jnp.bfloat16)
    mlp_term = jnp.dot(mlp_hidden, w_mlp_down, preferred_element_type=jnp.float32)
    attn_cols = jnp.dot(attended.astype(jnp.bfloat16), w_attn_out, preferred_element_type=jnp.float32)
    col_start = lax.axis_index("seq") * w_attn_out.shape[1]
    attn_term = lax.dynamic_update_slice(
        jnp.zeros((batch_rows, model_width), jnp.float32), attn_cols, (jnp.int32(0), col_start)
    )
    hidden_out = scatter_sum(devices, seq_size, ssm_term + mlp_term + attn_term, hidden_in)
    return (hidden_out, state_out)


def solution(mesh):
    placed = (
        P(None, ("grp", "seq")),
        P(),
        P(None, ("grp", "seq")),
        P(None, ("grp", "seq")),
        P(None, ("grp", "seq")),
        P(("grp", "seq")),
        P(None, None, ("grp", "seq")),
        P(("grp", "seq"), None),
        P(None, ("grp", "seq")),
        P(("grp", "seq")),
        P(None, ("grp", "seq")),
        P(("grp", "seq")),
        P(None, None, ("grp", "seq")),
        P(("grp", "seq"), None),
        P(None, "grp"),
        P(None, "grp"),
        P(None, "grp"),
        P("grp", "seq"),
        P(None, ("grp", "seq")),
        P(None, ("grp", "seq")),
        P(("grp", "seq"), None),
        P("seq", None, None),
        P(),
    )
    return jax.shard_map(
        functools.partial(per_device, mesh.size, mesh.shape["seq"]),
        mesh=mesh,
        in_specs=placed,
        out_specs=(P(None, ("grp", "seq")), P(None, None, ("grp", "seq"))),
        check_vma=False,
    )
```
